128 devices in a mesh: rows: 16 (over x, y_hi, core), cols: 8 (over y_lo, z).
Axes of the slice: x: 4, y: 4 (y_hi: 2, y_lo: 2; y = y_hi * 2 + y_lo), z: 4, core: 2. Of those that a mesh axis runs over, the one named last changes fastest.
Arguments:
- first_profiles: float32 [2048, 65536], P('rows', 'cols'), may hold values from -6 to 6
- second_profiles: float32 [256, 65536], P('rows', 'cols'), may hold values from -6 to 6
- pivot_ids: int32 [16], replicated, may hold values from 0 to 2047
- pivot_corr: float32 [16, 2048], P('cols', 'rows'), may hold values from -0.9 to 0.9
- pair_corr: float32 [2048, 256], P('rows'), may hold values from -0.9 to 0.9
Outputs:
- comoments: float32 [16, 2048, 256], P('cols', 'rows')
The draws below stay inside these ranges and needn't reach their ends.
All inputs are finite; a program needn't handle non-finite values.
Results may differ from the reference program's by a relative error of at most 0.00007.
Values sent between devices are 32-bit elements; how exact they have to be, the bound alone decides.
A program may use at most 64 MiB of HBM per device.

```python
import math
import jax
import jax.numpy as jnp
from jax import lax

NPIV = 16
NF = 2048
NS = 256
SAMPLES = 65536


def plant(entries, rng, low, high):
    spot = [jax.random.randint(jax.random.fold_in(rng, axis), (), 0, length) for axis, length in enumerate(entries.shape)]
    widest = entries.shape.index(max(entries.shape))
    beside = spot[:widest] + [(spot[widest] + 1) % entries.shape[widest]] + spot[widest + 1:]
    return entries.at[tuple(spot)].set(low).at[tuple(beside)].set(high)


def steps_of(stream_key, shape, split, smallest, largest):
    level = 1.0
    for axis_at, parts in split:
        draws = jax.random.uniform(jax.random.fold_in(jax.random.fold_in(stream_key, 6), axis_at), (parts,), jnp.float32, smallest / len(split), largest / len(split))
        level = level * jnp.repeat(jnp.exp(draws), shape[axis_at] // parts).reshape((-1,) + (1,) * (len(shape) - 1 - axis_at))
    return level


def gaussian(key, dims, deviation, most, cuts=(), dtype=jnp.bfloat16):
    drawn = deviation * jax.random.normal(key, dims, jnp.float32)
    if cuts:
        drawn = drawn * steps_of(key, dims, cuts, -0.22, 0.18)
    return jnp.clip(drawn, -most, most).astype(dtype)


def setup_inputs(seed: int = 0) -> dict:
    arg_keys = jax.random.split(jax.random.key(seed), 6)
    return {
        "first_profiles": gaussian(arg_keys[0], (NF, SAMPLES), 1.0, 6.0, ((0, 16), (1, 8)), jnp.float32),
        "second_profiles": gaussian(arg_keys[1], (NS, SAMPLES), 1.0, 6.0, ((0, 16), (1, 8)), jnp.float32),
        "pivot_ids": plant(jax.random.randint(arg_keys[2], (NPIV,), 0, NF), jax.random.fold_in(arg_keys[2], 1), 0, NF - 1).astype(jnp.int32),
        "pivot_corr": jnp.clip(jax.random.uniform(arg_keys[3], (NPIV, NF), jnp.float32, -0.9, 0.9) * steps_of(arg_keys[3], (NPIV, NF), ((0, 8), (1, 16)), -0.4, 0.0), -0.9, 0.9),
        "pair_corr": jnp.clip(jax.random.uniform(arg_keys[4], (NF, NS), jnp.float32, -0.9, 0.9) * steps_of(arg_keys[4], (NF, NS), ((0, 16),), -0.4, 0.0), -0.9, 0.9),
    }


def reference(first_profiles, second_profiles, pivot_ids, pivot_corr, pair_corr):
    pivots = jnp.take(first_profiles, pivot_ids, axis=0)
    root_count = math.sqrt(float(SAMPLES))

    def one_pivot(items):
        profile, corr_row = items
        scaled = first_profiles * profile[None, :]
        triple = lax.dot_general(scaled, second_profiles, (((1,), (1,)), ((), ())), precision=lax.Precision.HIGHEST, preferred_element_type=jnp.float32)
        return triple / (root_count * jnp.sqrt(1.0 + corr_row[:, None] ** 2 + pair_corr ** 2))
    return lax.map(one_pivot, (pivots, pivot_corr))
```

```python
import functools
import math

import jax
import jax.numpy as jnp
from jax import lax
from jax.experimental import pallas as pl
from jax.experimental.pallas import tpu as pltpu
from jax.sharding import PartitionSpec as P

MESH = pl.DeviceIdType.MESH
F32 = jnp.float32
BF16 = jnp.bfloat16
NT = (((1,), (1,)), ((), ()))
CHUNKS = 8
PIECES = 4
ORDER = (2, 1, 3, 0)


def halves(x):
    high = x.astype(BF16)
    return high, (x - high.astype(F32)).astype(BF16)


def kernel(
    root,
    ids,
    first_hbm,
    second_hbm,
    corr_ref,
    pair_ref,
    out_ref,
    first,
    blocks,
    high,
    low,
    scaled,
    tot,
    hop1,
    hop2,
    hop3,
    part,
    norm,
    mine,
    other,
    merged,
    gathered,
    pivots,
    load_f,
    load_s,
    s_send,
    s_recv,
    p_send,
    p_recv,
    r_send,
    r_recv,
):
    r, c = lax.axis_index("rows"), lax.axis_index("cols")
    core, chip = r % 2, r // 2
    x, y = chip // 2, chip % 2
    z, w = c % 4, c // 4
    rows, samples = first_hbm.shape
    size = samples // CHUNKS
    piece = samples // PIECES

    def at_chip(other_chip, other_core=None):
        return (other_chip * 2 + (core if other_core is None else other_core), c)

    x_up, x_down, x_far = (x + 1) % 4, (x + 3) % 4, (x + 2) % 4
    to_y = at_chip(x * 2 + 1 - y)
    to_up = at_chip(x_up * 2 + y)
    to_down = at_chip(x_down * 2 + y)
    to_core = at_chip(chip, 1 - core)
    z_up = (r, w * 4 + (z + 1) % 4)
    z_down = (r, w * 4 + (z + 3) % 4)
    to_w = (r, (1 - w) * 4 + z)

    def part_of(q):
        return pl.ds(pl.multiple_of(q * piece, 128), piece)

    def chunk_of(t):
        return pl.ds(pl.multiple_of(t * size, 128), size)

    def get_first(q):
        return pltpu.make_async_copy(
            first_hbm.at[:, part_of(q)], first.at[:, part_of(q)], load_f.at[q]
        )

    def get_second(t):
        return pltpu.make_async_copy(
            second_hbm.at[:, chunk_of(t)], blocks.at[t, core, x, y], load_s.at[t]
        )

    for q in range(PIECES):
        get_first(q).start()
    for t in range(CHUNKS):
        get_second(t).start()

    barrier = pltpu.get_barrier_semaphore()
    peers = [at_chip((chip + i) % 8) for i in range(1, 8)] + [to_core, z_up, z_down, to_w]
    for peer in peers:
        pl.semaphore_signal(barrier, inc=1, device_id=peer, device_id_type=MESH)
    pl.semaphore_wait(barrier, len(peers))

    def s_copy(t, n, ref, peer):
        return pltpu.make_async_remote_copy(
            src_ref=ref,
            dst_ref=ref,
            send_sem=s_send.at[t, n],
            recv_sem=s_recv.at[t, n],
            device_id=peer,
            device_id_type=MESH,
        )

    def s_copies(t):
        own = blocks.at[t, core, x, y]
        pair = blocks.at[t, core, x, 1 - y]
        return (
            s_copy(t, 0, own, to_y),
            s_copy(t, 1, own, to_up),
            s_copy(t, 2, own, to_down),
            s_copy(t, 3, pair, to_up),
            s_copy(t, 4, pair, to_down),
            s_copy(t, 5, blocks.at[t, core, x_down, y], to_up),
            s_copy(t, 6, blocks.at[t, core, x_up, 1 - y], to_down),
            s_copy(t, 7, blocks.at[t, core, x], to_core),
            s_copy(t, 8, blocks.at[t, core, x_down], to_core),
            s_copy(t, 9, blocks.at[t, core, x_up], to_core),
            s_copy(t, 10, blocks.at[t, core, x_far], to_core),
        )

    def s_stage(t, stage):
        copies = s_copies(t)
        if stage == 0:
            get_second(t).wait()
        waits = ((), (0,), (1, 3, 2, 4), (5, 6), (7, 8, 9, 10))[stage]
        starts = ((0, 1, 2), (3, 4, 7), (5, 6, 8, 9), (10,), ())[stage]
        for n in waits:
            copies[n].wait_recv()
        for n in starts:
            copies[n].start()

    def p_copy(q, n, src, dst, peer):
        return pltpu.make_async_remote_copy(
            src_ref=src,
            dst_ref=dst,
            send_sem=p_send.at[q, n],
            recv_sem=p_recv.at[q, n],
            device_id=peer,
            device_id_type=MESH,
        )

    def p_copies(q):
        span = part_of(q)
        first_copy = p_copy(
            q, 0, mine.at[pl.ds(8 * (1 - core), 8), :, span], other.at[:, :, span], to_core
        )
        spread, gather = [], []
        for i in range(1, 8):
            there = (chip + i) % 8
            spread.append(
                p_copy(q, i, merged.at[there, :, span], gathered.at[i, :, span], at_chip(there))
            )
            row = pivots.at[8 * core + chip, :, span]
            gather.append(p_copy(q, 7 + i, row, row, at_chip(there)))
        rows_here = pivots.at[pl.ds(8 * core, 8), :, span]
        last = p_copy(q, 15, rows_here, rows_here, to_core)
        return first_copy, spread, gather, last

    def p_stage(q, stage):
        first_copy, spread, gather, last = p_copies(q)
        span = part_of(q)
        if stage == 0:
            for j in range(16):
                spot = ids[j] - r * rows
                here = jnp.logical_and(spot >= 0, spot < rows)
                row = first[pl.ds(jnp.clip(spot, 0, rows - 1), 1), span]
                mine[j, :, span] = jnp.where(here, row, jnp.zeros_like(row))
            first_copy.start()
        elif stage == 1:
            first_copy.wait_recv()
            merged[:, :, span] = mine[pl.ds(8 * core, 8), :, span] + other[:, :, span]
            for copy in spread:
                copy.start()
        elif stage == 2:
            for copy in spread:
                copy.wait_recv()
            total = merged[chip, :, span]
            for i in range(1, 8):
                total = total + gathered[i, :, span]
            pivots[8 * core + chip, :, span] = total
            for copy in gather:
                copy.start()
        elif stage == 3:
            for copy in gather:
                copy.wait_recv()
            last.start()
        else:
            last.wait_recv()

    s_stage(0, 0)
    for q in range(PIECES):
        get_first(q).wait()
    p_stage(0, 0)
    s_stage(1, 0)
    p_stage(0, 1)
    s_stage(0, 1)
    p_stage(0, 2)
    s_stage(2, 0)
    s_stage(1, 1)
    p_stage(1, 0)
    s_stage(0, 2)
    p_stage(0, 3)
    s_stage(3, 0)
    s_stage(2, 1)
    s_stage(1, 2)
    s_stage(0, 3)
    p_stage(1, 1)
    for p in range(2):
        column = jnp.transpose(jnp.broadcast_to(corr_ref[p : p + 1, :], (rows, rows)))
        column = jnp.concatenate([column] * (pair_ref.shape[1] // rows), 1)
        pair = pair_ref[...]
        norm[p] = 1.0 / (root * jnp.sqrt(1.0 + column * column + pair * pair))
    p_stage(1, 2)
    p_stage(0, 4)

    tot[...] = jnp.zeros_like(tot)

    def index_of(p, d, e):
        return 2 * (((w + e) % 2) * 4 + (z + d) % 4) + p

    def build(slot, t, js):
        span = chunk_of(t)
        for n, j in enumerate(js):
            up, down = halves(first[:, span] * pivots[j, :, span])
            scaled[slot, n * rows : (n + 1) * rows, :size] = up
            scaled[slot, n * rows : (n + 1) * rows, size:] = down

    def product(slot, t, count):
        left = scaled[slot, : count * rows]
        up, down = high[t], low[t]
        left = jnp.concatenate([left, left[:, :size]], 1)
        right = jnp.concatenate([up, up, down], 1)
        return lax.dot_general(left, right, NT, preferred_element_type=F32)

    def main(t, carry):
        for ahead, stage in ((4, 0), (3, 1), (2, 2), (1, 3)):

            @pl.when(t + ahead < CHUNKS)
            def _():
                s_stage(t + ahead, stage)

        q = t // 2

        @pl.when(jnp.logical_and(t % 2 == 0, q + 1 < PIECES))
        def _():
            p_stage(q + 1, 3)

        @pl.when(jnp.logical_and(t % 2 == 0, q + 2 < PIECES))
        def _():
            p_stage(q + 2, 0)

        @pl.when(jnp.logical_and(t % 2 == 1, q + 2 < PIECES))
        def _():
            p_stage(q + 2, 1)

        @pl.when(jnp.logical_and(t % 2 == 1, q + 1 < PIECES))
        def _():
            p_stage(q + 1, 4)

        s_stage(t, 4)
        for n in range(16):
            a, b, k = n // 4, (n // 2) % 2, n % 2
            up, down = halves(blocks[t, k, a, b])
            high[t, n * 16 : (n + 1) * 16, :] = up
            low[t, n * 16 : (n + 1) * 16, :] = down
        for g in range(2):
            ds = ORDER[2 * g : 2 * g + 2]
            build(g, t, [index_of(0, d, e) for d in ds for e in range(2)])
            result = product(g, t, 4)
            for m, d in enumerate(ds):
                for e in range(2):
                    lo = (2 * m + e) * rows
                    tot[0, d, e] += result[lo : lo + rows]

        @pl.when(jnp.logical_and(t % 2 == 1, q + 2 < PIECES))
        def _():
            p_stage(q + 2, 2)

        return carry

    lax.fori_loop(0, CHUNKS, main, 0)

    half = rows // 2

    def r_copy(p, n, src, dst, peer):
        return pltpu.make_async_remote_copy(
            src_ref=src,
            dst_ref=dst,
            send_sem=r_send.at[p, n],
            recv_sem=r_recv.at[p, n],
            device_id=peer,
            device_id_type=MESH,
        )

    def r_copies(p):
        return (
            r_copy(p, 0, tot.at[p, 2, :, pl.ds(0, half)], hop1.at[p, 0], z_up),
            r_copy(p, 1, tot.at[p, 2, :, pl.ds(half, half)], hop1.at[p, 1], z_down),
            r_copy(p, 2, tot.at[p, 1, 1], hop2.at[p, 0, 1], z_up),
            r_copy(p, 3, tot.at[p, 3, 1], hop2.at[p, 1, 1], z_down),
            r_copy(p, 4, tot.at[p, 1, 0], hop2.at[p, 0, 0], z_up),
            r_copy(p, 5, tot.at[p, 3, 0], hop2.at[p, 1, 0], z_down),
            r_copy(p, 6, part.at[p], hop3.at[p], to_w),
        )

    def far_out(p):
        copies = r_copies(p)
        copies[0].start()
        copies[1].start()

    def near_out(p, side):
        copies = r_copies(p)
        copies[side].wait_recv()
        d = (1, 3)[side]
        tot[p, d, :, side * half : (side + 1) * half] += hop1[p, side]
        copies[2 + side].start()
        copies[4 + side].start()

    def pair_out(p):
        copies = r_copies(p)
        copies[2].wait_recv()
        copies[3].wait_recv()
        part[p] = tot[p, 0, 1] + hop2[p, 0, 1] + hop2[p, 1, 1]
        copies[6].start()

    def finish(p):
        copies = r_copies(p)
        copies[4].wait_recv()
        copies[5].wait_recv()
        mine_now = tot[p, 0, 0] + hop2[p, 0, 0] + hop2[p, 1, 0]
        copies[6].wait_recv()
        out_ref[p] = (mine_now + hop3[p]) * norm[p]

    def second_pass(d):
        js = [index_of(1, d, e) for e in range(2)]

        def body(u, carry):
            for g in range(2):
                t = 2 * u + g
                build(g, t, js)
                result = product(g, t, 2)
                for e in range(2):
                    tot[1, d, e] += result[e * rows : (e + 1) * rows]
            return carry

        lax.fori_loop(0, CHUNKS // 2, body, 0)

    far_out(0)
    second_pass(2)
    near_out(0, 0)
    near_out(0, 1)
    far_out(1)
    second_pass(1)
    near_out(1, 0)
    second_pass(3)
    near_out(1, 1)
    pair_out(0)
    second_pass(0)
    pair_out(1)
    finish(0)
    finish(1)

    def drain(t, carry):
        for copy in s_copies(t):
            copy.wait_send()
        return carry

    lax.fori_loop(0, CHUNKS, drain, 0)

    def drain_pivots(q, carry):
        first_copy, spread, gather, last = p_copies(q)
        for copy in (first_copy, *spread, *gather, last):
            copy.wait_send()
        return carry

    lax.fori_loop(0, PIECES, drain_pivots, 0)
    for p in range(2):
        for copy in r_copies(p):
            copy.wait_send()


def shards(first_profiles, second_profiles, pivot_ids, pivot_corr, pair_corr):
    n_cols = lax.axis_size("cols")
    rows, samples = first_profiles.shape
    second_rows = second_profiles.shape[0]
    width = pair_corr.shape[1]
    size = samples // CHUNKS
    root = math.sqrt(float(samples * n_cols))
    vmem = pl.BlockSpec(memory_space=pltpu.VMEM)
    hbm = pl.BlockSpec(memory_space=pl.ANY)
    dma = pltpu.SemaphoreType.DMA
    return pl.pallas_call(
        functools.partial(kernel, root),
        out_shape=jax.ShapeDtypeStruct((2, rows, width), F32),
        in_specs=[pl.BlockSpec(memory_space=pltpu.SMEM), hbm, hbm, vmem, vmem],
        out_specs=vmem,
        scratch_shapes=[
            pltpu.VMEM((rows, samples), F32),
            pltpu.VMEM((CHUNKS, 2, 4, 2, second_rows, size), F32),
            pltpu.VMEM((CHUNKS, width, size), BF16),
            pltpu.VMEM((CHUNKS, width, size), BF16),
            pltpu.VMEM((2, 4 * rows, 2 * size), BF16),
            pltpu.VMEM((2, 4, 2, rows, width), F32),
            pltpu.VMEM((2, 2, 2, rows // 2, width), F32),
            pltpu.VMEM((2, 2, 2, rows, width), F32),
            pltpu.VMEM((2, rows, width), F32),
            pltpu.VMEM((2, rows, width), F32),
            pltpu.VMEM((2, rows, width), F32),
            pltpu.VMEM((16, 1, samples), F32),
            pltpu.VMEM((8, 1, samples), F32),
            pltpu.VMEM((8, 1, samples), F32),
            pltpu.VMEM((8, 1, samples), F32),
            pltpu.VMEM((16, 1, samples), F32),
            dma((PIECES,)),
            dma((CHUNKS,)),
            dma((CHUNKS, 11)),
            dma((CHUNKS, 11)),
            dma((PIECES, 16)),
            dma((PIECES, 16)),
            dma((2, 7)),
            dma((2, 7)),
        ],
        compiler_params=pltpu.CompilerParams(
            collective_id=0, has_side_effects=True, vmem_limit_bytes=56 * 2**20
        ),
        name="comoments",
    )(pivot_ids, first_profiles, second_profiles, pivot_corr, pair_corr)


def solution(mesh):
    in_specs = (P("rows", "cols"), P("rows", "cols"), P(), P("cols", "rows"), P("rows", None))
    out_specs = P("cols", "rows", None)
    return jax.shard_map(shards, mesh=mesh, in_specs=in_specs, out_specs=out_specs, check_vma=False)
```

```python
import functools
import math

import jax
import jax.numpy as jnp
from jax import lax
from jax.experimental import pallas as pl
from jax.experimental.pallas import tpu as pltpu
from jax.sharding import PartitionSpec as P

MESH = pl.DeviceIdType.MESH
F32 = jnp.float32
BF16 = jnp.bfloat16
NT = (((1,), (1,)), ((), ()))
CHUNKS = 8
SMALL = 16
LAGS = ((0, 0), (3, 2), (3, 1), (6, 3), (7, 4), (8, 5), (10, 6))
AHEAD = 10
OPENING = (
    *(0, 1, 2, (), (0, 0), (1, 0), (0, 1), (1, 1), (0,), 3),
    *((0, 2), 4, 5, (0, 3), (1, 2), 6, 7, (0, 4), (1, 3)),
    *(8, (0, 5), 9, (0, 6)),
)
GROUP = (0, 1, 1, 2, 2, 3, 3, 4, 4, 4, 4, 5, 4)
PARTS = ((0, 2), (2, 6))
EARLY = (((0, 2), (0, 1)), ((0, 3), (0, 0)), ((1, 2), (1, 3)))


def halves(x):
    high = x.astype(BF16)
    return high, (x - high.astype(F32)).astype(BF16)


def kernel(
    root,
    ids,
    first_hbm,
    second_hbm,
    corr_ref,
    pair_ref,
    out_hbm,
    first,
    blocks,
    high,
    low,
    scaled,
    tot,
    hop1,
    hop2,
    side,
    far_side,
    part,
    norm,
    mine,
    other,
    merged,
    second,
    near,
    gathered,
    pivots,
    load_f,
    load_s,
    s_send,
    s_recv,
    p_send,
    p_recv,
    r_send,
    r_recv,
):
    r, c = lax.axis_index("rows"), lax.axis_index("cols")
    core, chip = r % 2, r // 2
    x, y = chip // 2, chip % 2
    z, w = c % 4, c // 4
    rows, samples = first_hbm.shape
    size = samples // CHUNKS
    small = samples // SMALL

    def at_chip(other_chip, other_core=None):
        return (other_chip * 2 + (core if other_core is None else other_core), c)

    x_up, x_down, x_far = (x + 1) % 4, (x + 3) % 4, (x + 2) % 4
    to_y = at_chip(x * 2 + 1 - y)
    to_up = at_chip(x_up * 2 + y)
    to_down = at_chip(x_down * 2 + y)
    to_core = at_chip(chip, 1 - core)
    z_up = (r, w * 4 + (z + 1) % 4)
    z_down = (r, w * 4 + (z + 3) % 4)
    to_w = (r, (1 - w) * 4 + z)

    def part_of(q):
        return pl.ds(PARTS[q][0] * size, PARTS[q][1] * size)

    def chunk_of(t):
        return pl.ds(pl.multiple_of(t * size, 128), size)

    def get_first():
        return pltpu.make_async_copy(first_hbm, first, load_f.at[0])

    def get_second(t):
        return pltpu.make_async_copy(
            second_hbm.at[:, pl.ds(pl.multiple_of(t * small, 128), small)], blocks.at[t, core, x, y], load_s.at[0]
        )

    for t in range(SMALL):
        get_second(t).start()
    get_first().start()

    barrier = pltpu.get_barrier_semaphore()
    to_far = at_chip(x_far * 2 + y)
    peers = [to_core, to_y, to_up, to_down, to_far, z_up, z_down, to_w]
    for peer in peers:
        pl.semaphore_signal(barrier, inc=1, device_id=peer, device_id_type=MESH)

    def s_copy(t, n, ref, peer):
        return pltpu.make_async_remote_copy(
            src_ref=ref,
            dst_ref=ref,
            send_sem=s_send.at[t // 8],
            recv_sem=s_recv.at[t, GROUP[n]],
            device_id=peer,
            device_id_type=MESH,
        )

    def s_copies(t):
        own = blocks.at[t, core, x, y]
        pair = blocks.at[t, core, x, 1 - y]
        far = blocks.at[t, core, x_far, y]
        half = own.shape[0] // 2
        return (
            s_copy(t, 0, own, to_y),
            s_copy(t, 1, own, to_up),
            s_copy(t, 2, own, to_down),
            s_copy(t, 3, pair, to_up),
            s_copy(t, 4, pair, to_down),
            s_copy(t, 5, blocks.at[t, core, x_down, y, pl.ds(0, half)], to_up),
            s_copy(t, 6, blocks.at[t, core, x_up, y, pl.ds(half, half)], to_down),
            s_copy(t, 7, blocks.at[t, core, x], to_core),
            s_copy(t, 8, blocks.at[t, core, x_down], to_core),
            s_copy(t, 9, blocks.at[t, core, x_up], to_core),
            s_copy(t, 10, far, to_core),
            s_copy(t, 11, far, to_y),
            s_copy(t, 12, blocks.at[t, core, x_far, 1 - y], to_core),
        )

    def s_stage(t, stage):
        copies = s_copies(t)
        starts = ((0, 1, 2), (3, 4, 7), (5, 6), (11, 10), (8, 9), (12,), ())[stage]
        landed = (
            None,
            (0, blocks.at[t, core, x, 1 - y]),
            (1, blocks.at[t, core, x]),
            (5, blocks.at[t, core, x_far, y]),
            (3, blocks.at[t, core, x]),
            (11, blocks.at[t, core, x_far, 1 - y]),
            (7, blocks.at[t, 1 - core]),
        )[stage]
        if landed:
            s_copy(t, *landed, to_core).wait_recv()
        for n in starts:
            copies[n].start()

    def turn(n):
        for lag, stage in LAGS:
            t = n - lag
            if isinstance(t, int):
                if 0 <= t < SMALL:
                    s_stage(t, stage)
            else:

                @pl.when(jnp.logical_and(t >= 0, t < SMALL))
                def _():
                    s_stage(t, stage)

    def p_copy(q, n, src, dst, peer):
        return pltpu.make_async_remote_copy(
            src_ref=src,
            dst_ref=dst,
            send_sem=p_send.at[0],
            recv_sem=p_recv.at[q, n],
            device_id=peer,
            device_id_type=MESH,
        )

    def p_copies(q):
        span = part_of(q)
        spread, gather = [], []
        row = pivots.at[8 * core + 4 * y + x, :, span]
        for i in range(1, 4):
            there = (x + i) % 4
            peer = at_chip(there * 2 + y)
            spread.append(p_copy(q, 2, near.at[there, :, span], gathered.at[i, :, span], peer))
            gather.append(p_copy(q, 3, row, row, peer))
        pair_rows = pivots.at[pl.ds(8 * core + 4 * y, 4), :, span]
        core_rows = pivots.at[pl.ds(8 * core, 8), :, span]
        return (
            [p_copy(q, 0, mine.at[pl.ds(8 * (1 - core), 8), :, span], other.at[:, :, span], to_core)],
            [p_copy(q, 1, merged.at[pl.ds(4 * (1 - y), 4), :, span], second.at[:, :, span], to_y)],
            spread,
            gather,
            [p_copy(q, 4, pair_rows, pair_rows, to_y)],
            [p_copy(q, 5, core_rows, core_rows, to_core)],
        )

    def p_stage(q, stage):
        copies = p_copies(q)
        span = part_of(q)
        if stage > 0:
            if stage in (3, 4):
                three = gathered.at[pl.ds(1, 3), :, span]
                p_copy(q, stage - 1, three, three, to_core).wait_recv()
            else:
                copies[stage - 1][0].wait_recv()
        if stage == 1:
            merged[:, :, span] = mine[pl.ds(8 * core, 8), :, span] + other[:, :, span]
        elif stage == 2:
            near[:, :, span] = merged[pl.ds(4 * y, 4), :, span] + second[:, :, span]
        elif stage == 3:
            total = near[x, :, span]
            for i in range(1, 4):
                total = total + gathered[i, :, span]
            pivots[8 * core + 4 * y + x, :, span] = total
        if stage < 6:
            for copy in copies[stage]:
                copy.start()

    def prepare():
        tot[...] = jnp.zeros_like(tot)
        for p in range(2):
            column = jnp.transpose(jnp.broadcast_to(corr_ref[p : p + 1, :], (rows, rows)))
            column = jnp.concatenate([column] * (pair_ref.shape[1] // rows), 1)
            pair = pair_ref[...]
            norm[p] = 1.0 / (root * jnp.sqrt(1.0 + column * column + pair * pair))

    def pick():
        get_first().wait()
        for q in range(2):
            span = part_of(q)
            for j in range(16):
                spot = ids[j] - r * rows
                here = jnp.logical_and(spot >= 0, spot < rows)
                row = first[pl.ds(jnp.clip(spot, 0, rows - 1), 1), span]
                mine[j, :, span] = jnp.where(here, row, jnp.zeros_like(row))

    pltpu.make_async_copy(blocks.at[0], blocks.at[0], load_s.at[0]).wait()
    pl.semaphore_wait(barrier, len(peers))

    for step in OPENING:
        if isinstance(step, int):
            turn(step)
        elif step == ():
            pick()
        elif step == (0,):
            prepare()
        else:
            p_stage(*step)

    def index_of(p, d, e):
        return 2 * (((w + e) % 2) * 4 + (z + d) % 4) + p

    def build(slot, t, js):
        span = chunk_of(t)
        for n, j in enumerate(js):
            up, down = halves(first[:, span] * pivots[j, :, span])
            scaled[slot, n * rows : (n + 1) * rows, :size] = up
            scaled[slot, n * rows : (n + 1) * rows, size:] = down

    def product(slot, t, count):
        left = scaled[slot, : count * rows]
        up, down = high[t], low[t]
        left = jnp.concatenate([left, left[:, :size]], 1)
        right = jnp.concatenate([up, up, down], 1)
        return lax.dot_general(left, right, NT, preferred_element_type=F32)

    def main(t, carry):
        turn(2 * t + AHEAD)
        turn(2 * t + AHEAD + 1)

        for when, stage in ((0, 4), (1, 5), (2, 6)):

            @pl.when(t == when)
            def _():
                p_stage(1, stage)

        for n in range(16):
            a, b, k = n // 4, (n // 2) % 2, n % 2
            for m in range(2):
                up, down = halves(blocks[2 * t + m, k, a, b])
                high[t, n * 16 : (n + 1) * 16, m * small : (m + 1) * small] = up
                low[t, n * 16 : (n + 1) * 16, m * small : (m + 1) * small] = down
        for g, group in enumerate(EARLY):
            build(g, t, [index_of(p, d, e) for p, d in group for e in range(2)])
            result = product(g, t, 2 * len(group))
            for m, (p, d) in enumerate(group):
                for e in range(2):
                    lo = (2 * m + e) * rows
                    tot[p, d, e] += result[lo : lo + rows]

        return carry

    lax.fori_loop(0, CHUNKS, main, 0)

    half = rows // 2

    def r_copy(p, n, src, dst, peer, lane=0):
        return pltpu.make_async_remote_copy(
            src_ref=src,
            dst_ref=dst,
            send_sem=r_send.at[p, lane],
            recv_sem=r_recv.at[p, n],
            device_id=peer,
            device_id_type=MESH,
        )

    def f_copies():
        return [r_copy(0, n, tot.at[0, d, 1], side.at[d], to_w) for n, d in enumerate((2, 3, 1, 0))] + [
            r_copy(0, 4, tot.at[0, 2, 0, pl.ds(0, half)], hop1.at[0, 0, 0], z_up, 1),
            r_copy(0, 5, tot.at[0, 2, 0, pl.ds(half, half)], hop1.at[0, 1, 0], z_down, 1),
            r_copy(0, 6, tot.at[0, 1, 0], hop2.at[0, 0, 0], z_up, 1),
            r_copy(0, 7, tot.at[0, 3, 0], hop2.at[0, 1, 0], z_down, 1),
        ]

    def r_copies():
        return (
            r_copy(1, 0, tot.at[1, 2, :, pl.ds(0, half)], hop1.at[1, 0], z_up),
            r_copy(1, 1, tot.at[1, 2, :, pl.ds(half, half)], hop1.at[1, 1], z_down),
            r_copy(1, 2, tot.at[1, 1, 1], hop2.at[1, 0, 1], z_up),
            r_copy(1, 3, tot.at[1, 3, 1], hop2.at[1, 1, 1], z_down),
            r_copy(1, 4, tot.at[1, 1, 0], hop2.at[1, 0, 0], z_up),
            r_copy(1, 5, tot.at[1, 3, 0], hop2.at[1, 1, 0], z_down),
            r_copy(1, 6, part, far_side, to_w, 1),
        )

    def fold_out():
        for copy in f_copies()[:4]:
            copy.start()

    def fold_in(n):
        d = (2, 3, 1, 0)[n]
        copies = f_copies()
        copies[n].wait_recv()
        tot[0, d, 0] += side[d]
        if n == 0:
            copies[4].start()
            copies[5].start()
        if n in (1, 2):
            way = 2 - n
            copies[4 + way].wait_recv()
            tot[0, d, 0, way * half : (way + 1) * half] += hop1[0, way, 0]
            copies[6 + way].start()

    def far_out():
        copies = r_copies()
        copies[0].start()
        copies[1].start()

    def near_out(way):
        copies = r_copies()
        copies[way].wait_recv()
        d = (1, 3)[way]
        tot[1, d, :, way * half : (way + 1) * half] += hop1[1, way]
        copies[2 + way].start()
        copies[4 + way].start()

    def pair_out():
        copies = r_copies()
        copies[2].wait_recv()
        copies[3].wait_recv()
        part[...] = tot[1, 0, 1] + hop2[1, 0, 1] + hop2[1, 1, 1]
        copies[6].start()

    def put_out(p):
        return pltpu.make_async_copy(norm.at[p], out_hbm.at[p], load_f.at[p])

    def finish(p):
        copies = (f_copies(), r_copies())[p]
        for n in ((6, 7), (4, 5))[p]:
            copies[n].wait_recv()
        total = tot[p, 0, 0] + hop2[p, 0, 0] + hop2[p, 1, 0]
        if p == 1:
            copies[6].wait_recv()
            total = total + far_side[...]
        norm[p] = total * norm[p]
        put_out(p).start()

    def second_pass(d):
        js = [index_of(1, d, e) for e in range(2)]

        def body(u, carry):
            for g in range(2):
                t = 2 * u + g
                build(g, t, js)
                result = product(g, t, 2)
                for e in range(2):
                    tot[1, d, e] += result[e * rows : (e + 1) * rows]
            return carry

        lax.fori_loop(0, CHUNKS // 2, body, 0)

    fold_out()
    far_out()
    second_pass(1)
    fold_in(0)
    near_out(0)
    near_out(1)
    second_pass(0)
    fold_in(1)
    fold_in(2)
    for t in (0, 8):
        all_sent = blocks.at[pl.ds(0, 15), 0]
        s_copy(t, 0, all_sent, to_core).wait_send()
    rows_sent = blocks.at[pl.ds(0, 15), 0, 0]
    p_copy(0, 0, rows_sent, rows_sent, to_core).wait_send()
    fold_in(3)
    pair_out()
    finish(0)
    finish(1)
    for p, lane, sent in (
        (0, 0, side),
        (0, 1, side.at[pl.ds(0, 3)]),
        (1, 0, tot.at[0, pl.ds(0, 3)]),
        (1, 1, part),
    ):
        r_copy(p, 0, sent, sent, to_core, lane).wait_send()
    for p in range(2):
        put_out(p).wait()


def shards(first_profiles, second_profiles, pivot_ids, pivot_corr, pair_corr):
    n_cols = lax.axis_size("cols")
    rows, samples = first_profiles.shape
    second_rows = second_profiles.shape[0]
    width = pair_corr.shape[1]
    size = samples // CHUNKS
    small = samples // SMALL
    root = math.sqrt(float(samples * n_cols))
    vmem = pl.BlockSpec(memory_space=pltpu.VMEM)
    hbm = pl.BlockSpec(memory_space=pl.ANY)
    dma = pltpu.SemaphoreType.DMA
    return pl.pallas_call(
        functools.partial(kernel, root),
        out_shape=jax.ShapeDtypeStruct((2, rows, width), F32),
        in_specs=[pl.BlockSpec(memory_space=pltpu.SMEM), hbm, hbm, vmem, vmem],
        out_specs=hbm,
        scratch_shapes=[
            pltpu.VMEM((rows, samples), F32),
            pltpu.VMEM((SMALL, 2, 4, 2, second_rows, small), F32),
            pltpu.VMEM((CHUNKS, width, size), BF16),
            pltpu.VMEM((CHUNKS, width, size), BF16),
            pltpu.VMEM((3, 4 * rows, 2 * size), BF16),
            pltpu.VMEM((2, 4, 2, rows, width), F32),
            pltpu.VMEM((2, 2, 2, rows // 2, width), F32),
            pltpu.VMEM((2, 2, 2, rows, width), F32),
            pltpu.VMEM((4, rows, width), F32),
            pltpu.VMEM((rows, width), F32),
            pltpu.VMEM((rows, width), F32),
            pltpu.VMEM((2, rows, width), F32),
            pltpu.VMEM((16, 1, samples), F32),
            pltpu.VMEM((8, 1, samples), F32),
            pltpu.VMEM((8, 1, samples), F32),
            pltpu.VMEM((4, 1, samples), F32),
            pltpu.VMEM((4, 1, samples), F32),
            pltpu.VMEM((4, 1, samples), F32),
            pltpu.VMEM((16, 1, samples), F32),
            dma((2,)),
            dma((1,)),
            dma((2,)),
            dma((SMALL, 6)),
            dma((1,)),
            dma((2, 6)),
            dma((2, 2)),
            dma((2, 8)),
        ],
        compiler_params=pltpu.CompilerParams(
            collective_id=0, has_side_effects=True, vmem_limit_bytes=56 * 2**20
        ),
        name="comoments",
    )(pivot_ids, first_profiles, second_profiles, pivot_corr, pair_corr)


def solution(mesh):
    in_specs = (P("rows", "cols"), P("rows", "cols"), P(), P("cols", "rows"), P("rows", None))
    out_specs = P("cols", "rows", None)
    return jax.shard_map(shards, mesh=mesh, in_specs=in_specs, out_specs=out_specs, check_vma=False)
```

```python
import functools
import math

import jax
import jax.numpy as jnp
from jax import lax
from jax.experimental import pallas as pl
from jax.experimental.pallas import tpu as pltpu
from jax.sharding import PartitionSpec as P

MESH = pl.DeviceIdType.MESH
F32 = jnp.float32
BF16 = jnp.bfloat16
NT = (((1,), (1,)), ((), ()))
CHUNKS = 8
SMALL = 16
LAGS = ((0, 0), (3, 2), (3, 1), (5, 3), (7, 4), (8, 5), (10, 6))
AHEAD = 10
OPENING = (
    *(0, 1, 2, (), (0, 0), (1, 0), (0, 1), (1, 1), (0,), 3),
    *((0, 2), 4, 5, (0, 3), (1, 2), 6, 7, (0, 4), (1, 3)),
    *(8, (0, 5), 9, (1, 4), (0, 6)),
)
GROUP = (0, 1, 1, 2, 2, 3, 3, 4, 4, 4, 4, 5, 4)
PARTS = ((0, 2), (2, 6))
EARLY = (((0, 2), (0, 1)), ((0, 3), (0, 0)), ((1, 2), (1, 3)))


def halves(x):
    high = x.astype(BF16)
    return high, (x - high.astype(F32)).astype(BF16)


def kernel(
    root,
    ids,
    first_hbm,
    second_hbm,
    corr_ref,
    pair_ref,
    out_hbm,
    first,
    blocks,
    high,
    low,
    scaled,
    tot,
    hop1,
    hop2,
    side,
    far_side,
    part,
    norm,
    mine,
    other,
    merged,
    second,
    near,
    gathered,
    pivots,
    load_f,
    load_s,
    s_send,
    s_recv,
    p_send,
    p_recv,
    r_send,
    r_recv,
):
    r, c = lax.axis_index("rows"), lax.axis_index("cols")
    core, chip = r % 2, r // 2
    x, y = chip // 2, chip % 2
    z, w = c % 4, c // 4
    rows, samples = first_hbm.shape
    size = samples // CHUNKS
    small = samples // SMALL

    def at_chip(other_chip, other_core=None):
        return (other_chip * 2 + (core if other_core is None else other_core), c)

    x_up, x_down, x_far = (x + 1) % 4, (x + 3) % 4, (x + 2) % 4
    to_y = at_chip(x * 2 + 1 - y)
    to_up = at_chip(x_up * 2 + y)
    to_down = at_chip(x_down * 2 + y)
    to_core = at_chip(chip, 1 - core)
    z_up = (r, w * 4 + (z + 1) % 4)
    z_down = (r, w * 4 + (z + 3) % 4)
    to_w = (r, (1 - w) * 4 + z)

    def part_of(q):
        return pl.ds(PARTS[q][0] * size, PARTS[q][1] * size)

    def chunk_of(t):
        return pl.ds(pl.multiple_of(t * size, 128), size)

    def get_first():
        return pltpu.make_async_copy(first_hbm, first, load_f.at[0])

    def get_second(t):
        return pltpu.make_async_copy(
            second_hbm.at[:, pl.ds(pl.multiple_of(t * small, 128), small)], blocks.at[t, core, x, y], load_s.at[0]
        )

    for t in range(SMALL):
        get_second(t).start()
    get_first().start()

    barrier = pltpu.get_barrier_semaphore()
    to_far = at_chip(x_far * 2 + y)
    peers = [to_core, to_y, to_up, to_down, to_far, z_up, z_down, to_w]
    for peer in peers:
        pl.semaphore_signal(barrier, inc=1, device_id=peer, device_id_type=MESH)

    def s_copy(t, n, ref, peer):
        return pltpu.make_async_remote_copy(
            src_ref=ref,
            dst_ref=ref,
            send_sem=s_send.at[t // 8],
            recv_sem=s_recv.at[t, GROUP[n]],
            device_id=peer,
            device_id_type=MESH,
        )

    def s_copies(t):
        own = blocks.at[t, core, x, y]
        pair = blocks.at[t, core, x, 1 - y]
        far = blocks.at[t, core, x_far, y]
        half = own.shape[0] // 2
        return (
            s_copy(t, 0, own, to_y),
            s_copy(t, 1, own, to_up),
            s_copy(t, 2, own, to_down),
            s_copy(t, 3, pair, to_up),
            s_copy(t, 4, pair, to_down),
            s_copy(t, 5, blocks.at[t, core, x_down, y, pl.ds(0, half)], to_up),
            s_copy(t, 6, blocks.at[t, core, x_up, y, pl.ds(half, half)], to_down),
            s_copy(t, 7, blocks.at[t, core, x], to_core),
            s_copy(t, 8, blocks.at[t, core, x_down], to_core),
            s_copy(t, 9, blocks.at[t, core, x_up], to_core),
            s_copy(t, 10, far, to_core),
            s_copy(t, 11, far, to_y),
            s_copy(t, 12, blocks.at[t, core, x_far, 1 - y], to_core),
        )

    def s_stage(t, stage):
        copies = s_copies(t)
        starts = ((0, 1, 2), (3, 4, 7), (5, 6), (11, 10), (8, 9), (12,), ())[stage]
        landed = (
            None,
            (0, blocks.at[t, core, x, 1 - y]),
            (1, blocks.at[t, core, x]),
            (5, blocks.at[t, core, x_far, y]),
            (3, blocks.at[t, core, x]),
            (11, blocks.at[t, core, x_far, 1 - y]),
            (7, blocks.at[t, 1 - core]),
        )[stage]
        if landed:
            s_copy(t, *landed, to_core).wait_recv()
        for n in starts:
            copies[n].start()

    def turn(n):
        for lag, stage in LAGS:
            t = n - lag
            if isinstance(t, int):
                if 0 <= t < SMALL:
                    s_stage(t, stage)
            else:

                @pl.when(jnp.logical_and(t >= 0, t < SMALL))
                def _():
                    s_stage(t, stage)

    def p_copy(q, n, src, dst, peer):
        return pltpu.make_async_remote_copy(
            src_ref=src,
            dst_ref=dst,
            send_sem=p_send.at[0],
            recv_sem=p_recv.at[q, n],
            device_id=peer,
            device_id_type=MESH,
        )

    def p_copies(q):
        span = part_of(q)
        spread, gather = [], []
        row = pivots.at[8 * core + 4 * y + x, :, span]
        for i in range(1, 4):
            there = (x + i) % 4
            peer = at_chip(there * 2 + y)
            spread.append(p_copy(q, 2, near.at[there, :, span], gathered.at[i, :, span], peer))
            gather.append(p_copy(q, 3, row, row, peer))
        pair_rows = pivots.at[pl.ds(8 * core + 4 * y, 4), :, span]
        core_rows = pivots.at[pl.ds(8 * core, 8), :, span]
        return (
            [p_copy(q, 0, mine.at[pl.ds(8 * (1 - core), 8), :, span], other.at[:, :, span], to_core)],
            [p_copy(q, 1, merged.at[pl.ds(4 * (1 - y), 4), :, span], second.at[:, :, span], to_y)],
            spread,
            gather,
            [p_copy(q, 4, pair_rows, pair_rows, to_y)],
            [p_copy(q, 5, core_rows, core_rows, to_core)],
        )

    def p_stage(q, stage):
        copies = p_copies(q)
        span = part_of(q)
        if stage > 0:
            if stage in (3, 4):
                three = gathered.at[pl.ds(1, 3), :, span]
                p_copy(q, stage - 1, three, three, to_core).wait_recv()
            else:
                copies[stage - 1][0].wait_recv()
        if stage == 1:
            merged[:, :, span] = mine[pl.ds(8 * core, 8), :, span] + other[:, :, span]
        elif stage == 2:
            near[:, :, span] = merged[pl.ds(4 * y, 4), :, span] + second[:, :, span]
        elif stage == 3:
            total = near[x, :, span]
            for i in range(1, 4):
                total = total + gathered[i, :, span]
            pivots[8 * core + 4 * y + x, :, span] = total
        if stage < 6:
            for copy in copies[stage]:
                copy.start()

    def prepare():
        tot[...] = jnp.zeros_like(tot)
        for p in range(2):
            column = jnp.transpose(jnp.broadcast_to(corr_ref[p : p + 1, :], (rows, rows)))
            column = jnp.concatenate([column] * (pair_ref.shape[1] // rows), 1)
            pair = pair_ref[...]
            norm[p] = 1.0 / (root * jnp.sqrt(1.0 + column * column + pair * pair))

    def pick():
        get_first().wait()
        for q in range(2):
            span = part_of(q)
            for j in range(16):
                spot = ids[j] - r * rows
                here = jnp.logical_and(spot >= 0, spot < rows)
                row = first[pl.ds(jnp.clip(spot, 0, rows - 1), 1), span]
                mine[j, :, span] = jnp.where(here, row, jnp.zeros_like(row))

    pltpu.make_async_copy(blocks.at[0], blocks.at[0], load_s.at[0]).wait()
    pl.semaphore_wait(barrier, len(peers))

    for step in OPENING:
        if isinstance(step, int):
            turn(step)
        elif step == ():
            pick()
        elif step == (0,):
            prepare()
        else:
            p_stage(*step)

    def index_of(p, d, e):
        return 2 * (((w + e) % 2) * 4 + (z + d) % 4) + p

    def build(slot, t, js):
        span = chunk_of(t)
        for n, j in enumerate(js):
            up, down = halves(first[:, span] * pivots[j, :, span])
            scaled[slot, n * rows : (n + 1) * rows, :size] = up
            scaled[slot, n * rows : (n + 1) * rows, size:] = down

    def product(slot, t, count):
        left = scaled[slot, : count * rows]
        up, down = high[t], low[t]
        left = jnp.concatenate([left, left[:, :size]], 1)
        right = jnp.concatenate([up, up, down], 1)
        return lax.dot_general(left, right, NT, preferred_element_type=F32)

    def main(t, carry):
        turn(2 * t + AHEAD)
        turn(2 * t + AHEAD + 1)

        for when, stage in ((1, 5), (2, 6)):

            @pl.when(t == when)
            def _():
                p_stage(1, stage)

        for n in range(16):
            a, b, k = n // 4, (n // 2) % 2, n % 2
            for m in range(2):
                up, down = halves(blocks[2 * t + m, k, a, b])
                high[t, n * 16 : (n + 1) * 16, m * small : (m + 1) * small] = up
                low[t, n * 16 : (n + 1) * 16, m * small : (m + 1) * small] = down
        for g, group in enumerate(EARLY):
            build(g, t, [index_of(p, d, e) for p, d in group for e in range(2)])
            result = product(g, t, 2 * len(group))
            for m, (p, d) in enumerate(group):
                for e in range(2):
                    lo = (2 * m + e) * rows
                    tot[p, d, e] += result[lo : lo + rows]

        return carry

    lax.fori_loop(0, CHUNKS, main, 0)

    half = rows // 2

    def r_copy(p, n, src, dst, peer, lane=0):
        return pltpu.make_async_remote_copy(
            src_ref=src,
            dst_ref=dst,
            send_sem=r_send.at[p, lane],
            recv_sem=r_recv.at[p, n],
            device_id=peer,
            device_id_type=MESH,
        )

    def f_copies():
        return [r_copy(0, n, tot.at[0, d, 1], side.at[d], to_w) for n, d in enumerate((2, 3, 1, 0))] + [
            r_copy(0, 4, tot.at[0, 2, 0, pl.ds(0, half)], hop1.at[0, 0, 0], z_up, 1),
            r_copy(0, 5, tot.at[0, 2, 0, pl.ds(half, half)], hop1.at[0, 1, 0], z_down, 1),
            r_copy(0, 6, tot.at[0, 1, 0], hop2.at[0, 0, 0], z_up, 1),
            r_copy(0, 7, tot.at[0, 3, 0], hop2.at[0, 1, 0], z_down, 1),
        ]

    def r_copies():
        return (
            r_copy(1, 0, tot.at[1, 2, :, pl.ds(0, half)], hop1.at[1, 0], z_up),
            r_copy(1, 1, tot.at[1, 2, :, pl.ds(half, half)], hop1.at[1, 1], z_down),
            r_copy(1, 2, tot.at[1, 1, 1], hop2.at[1, 0, 1], z_up),
            r_copy(1, 3, tot.at[1, 3, 1], hop2.at[1, 1, 1], z_down),
            r_copy(1, 4, tot.at[1, 1, 0], hop2.at[1, 0, 0], z_up),
            r_copy(1, 5, tot.at[1, 3, 0], hop2.at[1, 1, 0], z_down),
            r_copy(1, 6, part, far_side, to_w, 1),
        )

    def fold_out():
        for copy in f_copies()[:4]:
            copy.start()

    def fold_in(n):
        d = (2, 3, 1, 0)[n]
        copies = f_copies()
        copies[n].wait_recv()
        tot[0, d, 0] += side[d]
        if n == 0:
            copies[4].start()
            copies[5].start()
        if n in (1, 2):
            way = 2 - n
            copies[4 + way].wait_recv()
            tot[0, d, 0, way * half : (way + 1) * half] += hop1[0, way, 0]
            copies[6 + way].start()

    def far_out():
        copies = r_copies()
        copies[0].start()
        copies[1].start()

    def near_out(way):
        copies = r_copies()
        copies[way].wait_recv()
        d = (1, 3)[way]
        tot[1, d, :, way * half : (way + 1) * half] += hop1[1, way]
        copies[2 + way].start()
        copies[4 + way].start()

    def pair_out():
        copies = r_copies()
        copies[2].wait_recv()
        copies[3].wait_recv()
        part[...] = tot[1, 0, 1] + hop2[1, 0, 1] + hop2[1, 1, 1]
        copies[6].start()

    def put_out(p):
        return pltpu.make_async_copy(norm.at[p], out_hbm.at[p], load_f.at[p])

    def finish(p):
        copies = (f_copies(), r_copies())[p]
        for n in ((6, 7), (4, 5))[p]:
            copies[n].wait_recv()
        total = tot[p, 0, 0] + hop2[p, 0, 0] + hop2[p, 1, 0]
        if p == 1:
            copies[6].wait_recv()
            total = total + far_side[...]
        norm[p] = total * norm[p]
        put_out(p).start()

    def second_pass(d):
        js = [index_of(1, d, e) for e in range(2)]

        def body(u, carry):
            for g in range(2):
                t = 2 * u + g
                build(g, t, js)
                result = product(g, t, 2)
                for e in range(2):
                    tot[1, d, e] += result[e * rows : (e + 1) * rows]
            return carry

        lax.fori_loop(0, CHUNKS // 2, body, 0)

    fold_out()
    far_out()
    second_pass(1)
    fold_in(0)
    near_out(0)
    near_out(1)
    second_pass(0)
    fold_in(1)
    fold_in(2)
    for t in (0, 8):
        all_sent = blocks.at[pl.ds(0, 15), 0]
        s_copy(t, 0, all_sent, to_core).wait_send()
    rows_sent = blocks.at[pl.ds(0, 15), 0, 0]
    p_copy(0, 0, rows_sent, rows_sent, to_core).wait_send()
    fold_in(3)
    pair_out()
    finish(0)
    finish(1)
    for p, lane, sent in (
        (0, 0, side),
        (0, 1, side.at[pl.ds(0, 3)]),
        (1, 0, tot.at[0, pl.ds(0, 3)]),
        (1, 1, part),
    ):
        r_copy(p, 0, sent, sent, to_core, lane).wait_send()
    for p in range(2):
        put_out(p).wait()


def shards(first_profiles, second_profiles, pivot_ids, pivot_corr, pair_corr):
    n_cols = lax.axis_size("cols")
    rows, samples = first_profiles.shape
    second_rows = second_profiles.shape[0]
    width = pair_corr.shape[1]
    size = samples // CHUNKS
    small = samples // SMALL
    root = math.sqrt(float(samples * n_cols))
    vmem = pl.BlockSpec(memory_space=pltpu.VMEM)
    hbm = pl.BlockSpec(memory_space=pl.ANY)
    dma = pltpu.SemaphoreType.DMA
    return pl.pallas_call(
        functools.partial(kernel, root),
        out_shape=jax.ShapeDtypeStruct((2, rows, width), F32),
        in_specs=[pl.BlockSpec(memory_space=pltpu.SMEM), hbm, hbm, vmem, vmem],
        out_specs=hbm,
        scratch_shapes=[
            pltpu.VMEM((rows, samples), F32),
            pltpu.VMEM((SMALL, 2, 4, 2, second_rows, small), F32),
            pltpu.VMEM((CHUNKS, width, size), BF16),
            pltpu.VMEM((CHUNKS, width, size), BF16),
            pltpu.VMEM((3, 4 * rows, 2 * size), BF16),
            pltpu.VMEM((2, 4, 2, rows, width), F32),
            pltpu.VMEM((2, 2, 2, rows // 2, width), F32),
            pltpu.VMEM((2, 2, 2, rows, width), F32),
            pltpu.VMEM((4, rows, width), F32),
            pltpu.VMEM((rows, width), F32),
            pltpu.VMEM((rows, width), F32),
            pltpu.VMEM((2, rows, width), F32),
            pltpu.VMEM((16, 1, samples), F32),
            pltpu.VMEM((8, 1, samples), F32),
            pltpu.VMEM((8, 1, samples), F32),
            pltpu.VMEM((4, 1, samples), F32),
            pltpu.VMEM((4, 1, samples), F32),
            pltpu.VMEM((4, 1, samples), F32),
            pltpu.VMEM((16, 1, samples), F32),
            dma((2,)),
            dma((1,)),
            dma((2,)),
            dma((SMALL, 6)),
            dma((1,)),
            dma((2, 6)),
            dma((2, 2)),
            dma((2, 8)),
        ],
        compiler_params=pltpu.CompilerParams(
            collective_id=0, has_side_effects=True, vmem_limit_bytes=56 * 2**20
        ),
        name="comoments",
    )(pivot_ids, first_profiles, second_profiles, pivot_corr, pair_corr)


def solution(mesh):
    in_specs = (P("rows", "cols"), P("rows", "cols"), P(), P("cols", "rows"), P("rows", None))
    out_specs = P("cols", "rows", None)
    return jax.shard_map(shards, mesh=mesh, in_specs=in_specs, out_specs=out_specs, check_vma=False)
```

```python
import functools
import math

import jax
import jax.numpy as jnp
from jax import lax
from jax.experimental import pallas as pl
from jax.experimental.pallas import tpu as pltpu
from jax.sharding import PartitionSpec as P

MESH = pl.DeviceIdType.MESH
F32 = jnp.float32
BF16 = jnp.bfloat16
NT = (((1,), (1,)), ((), ()))
CHUNKS = 8
SMALL = 16
LAGS = ((3, 2), (5, 3), (0, 0), (3, 1), (8, 4), (10, 5))
AHEAD = 10
OPENING = (
    *(0, 1, 2, (), (0, 0), (1, 0), (0, 1), (1, 1), (0,), 3),
    *((0, 2), 4, 5, (0, 3), (1, 2), 6, 7, (0, 4), (1, 3)),
    *(8, (0, 5), 9, (1, 4), (0, 6)),
)
GROUP = (0, 1, 1, 2, 2, 3, 3, 4, 5)
PARTS = ((0, 2), (2, 6))
EARLY = (((0, 2), (0, 1)), ((0, 3), (0, 0)), ((1, 2), (1, 3)))


def halves(x):
    high = x.astype(BF16)
    return high, (x - high.astype(F32)).astype(BF16)


def kernel(
    root,
    ids,
    first_hbm,
    second_hbm,
    corr_ref,
    pair_ref,
    out_hbm,
    first,
    blocks,
    high,
    low,
    scaled,
    tot,
    hop1,
    hop2,
    side,
    far_side,
    part,
    norm,
    mine,
    other,
    merged,
    second,
    near,
    gathered,
    pivots,
    load_f,
    load_s,
    s_send,
    s_recv,
    p_send,
    p_recv,
    r_send,
    r_recv,
):
    r, c = lax.axis_index("rows"), lax.axis_index("cols")
    core, chip = r % 2, r // 2
    x, y = chip // 2, chip % 2
    z, w = c % 4, c // 4
    rows, samples = first_hbm.shape
    size = samples // CHUNKS
    small = samples // SMALL

    def at_chip(other_chip, other_core=None):
        return (other_chip * 2 + (core if other_core is None else other_core), c)

    x_up, x_down, x_far = (x + 1) % 4, (x + 3) % 4, (x + 2) % 4
    to_y = at_chip(x * 2 + 1 - y)
    to_up = at_chip(x_up * 2 + y)
    to_down = at_chip(x_down * 2 + y)
    to_core = at_chip(chip, 1 - core)
    z_up = (r, w * 4 + (z + 1) % 4)
    z_down = (r, w * 4 + (z + 3) % 4)
    to_w = (r, (1 - w) * 4 + z)

    def part_of(q):
        return pl.ds(PARTS[q][0] * size, PARTS[q][1] * size)

    def chunk_of(t):
        return pl.ds(pl.multiple_of(t * size, 128), size)

    def get_first():
        return pltpu.make_async_copy(first_hbm, first, load_f.at[0])

    def get_second(t):
        return pltpu.make_async_copy(
            second_hbm.at[:, pl.ds(pl.multiple_of(t * small, 128), small)], blocks.at[t, core, x, y], load_s.at[0]
        )

    for t in range(SMALL):
        get_second(t).start()
    get_first().start()

    barrier = pltpu.get_barrier_semaphore()
    to_far = at_chip(x_far * 2 + y)
    peers = [to_core, to_y, to_up, to_down, to_far, z_up, z_down, to_w]
    for peer in peers:
        pl.semaphore_signal(barrier, inc=1, device_id=peer, device_id_type=MESH)

    def s_copy(t, n, ref, peer):
        return pltpu.make_async_remote_copy(
            src_ref=ref,
            dst_ref=ref,
            send_sem=s_send.at[t // 8],
            recv_sem=s_recv.at[t, GROUP[n]],
            device_id=peer,
            device_id_type=MESH,
        )

    def s_copies(t):
        own = blocks.at[t, core, x, y]
        pair = blocks.at[t, core, x, 1 - y]
        far = blocks.at[t, core, x_far, y]
        half = own.shape[0] // 2
        return (
            s_copy(t, 0, own, to_y),
            s_copy(t, 1, own, to_up),
            s_copy(t, 2, own, to_down),
            s_copy(t, 3, pair, to_up),
            s_copy(t, 4, pair, to_down),
            s_copy(t, 5, blocks.at[t, core, x_down, y, pl.ds(0, half)], to_up),
            s_copy(t, 6, blocks.at[t, core, x_up, y, pl.ds(half, half)], to_down),
            s_copy(t, 7, far, to_y),
            s_copy(t, 8, blocks.at[t, core], to_core),
        )

    def s_stage(t, stage):
        copies = s_copies(t)
        starts = ((0, 1, 2), (3, 4), (5, 6), (7,), (8,), ())[stage]
        landed = (
            (),
            ((0, blocks.at[t, core, x, 1 - y]),),
            ((1, blocks.at[t, core, x]),),
            ((5, blocks.at[t, core, x_far, y]),),
            ((3, blocks.at[t, core, x]), (7, blocks.at[t, core, x_far, 1 - y])),
            ((8, blocks.at[t, 1 - core]),),
        )[stage]
        for arrival in landed:
            s_copy(t, *arrival, to_core).wait_recv()
        for n in starts:
            copies[n].start()

    def turn(n):
        for lag, stage in LAGS:
            t = n - lag
            if isinstance(t, int):
                if 0 <= t < SMALL:
                    s_stage(t, stage)
            else:

                @pl.when(jnp.logical_and(t >= 0, t < SMALL))
                def _():
                    s_stage(t, stage)

    def p_copy(q, n, src, dst, peer):
        return pltpu.make_async_remote_copy(
            src_ref=src,
            dst_ref=dst,
            send_sem=p_send.at[0],
            recv_sem=p_recv.at[q, n],
            device_id=peer,
            device_id_type=MESH,
        )

    def p_copies(q):
        span = part_of(q)
        spread, gather = [], []
        row = pivots.at[8 * core + 4 * y + x, :, span]
        for i in range(1, 4):
            there = (x + i) % 4
            peer = at_chip(there * 2 + y)
            spread.append(p_copy(q, 2, near.at[there, :, span], gathered.at[i, :, span], peer))
            gather.append(p_copy(q, 3, row, row, peer))
        pair_rows = pivots.at[pl.ds(8 * core + 4 * y, 4), :, span]
        core_rows = pivots.at[pl.ds(8 * core, 8), :, span]
        return (
            [p_copy(q, 0, mine.at[pl.ds(8 * (1 - core), 8), :, span], other.at[:, :, span], to_core)],
            [p_copy(q, 1, merged.at[pl.ds(4 * (1 - y), 4), :, span], second.at[:, :, span], to_y)],
            spread,
            gather,
            [p_copy(q, 4, pair_rows, pair_rows, to_y)],
            [p_copy(q, 5, core_rows, core_rows, to_core)],
        )

    def p_stage(q, stage):
        copies = p_copies(q)
        span = part_of(q)
        if stage > 0:
            if stage in (3, 4):
                three = gathered.at[pl.ds(1, 3), :, span]
                p_copy(q, stage - 1, three, three, to_core).wait_recv()
            else:
                copies[stage - 1][0].wait_recv()
        if stage == 1:
            merged[:, :, span] = mine[pl.ds(8 * core, 8), :, span] + other[:, :, span]
        elif stage == 2:
            near[:, :, span] = merged[pl.ds(4 * y, 4), :, span] + second[:, :, span]
        elif stage == 3:
            total = near[x, :, span]
            for i in range(1, 4):
                total = total + gathered[i, :, span]
            pivots[8 * core + 4 * y + x, :, span] = total
        if stage < 6:
            for copy in copies[stage]:
                copy.start()

    def prepare():
        tot[...] = jnp.zeros_like(tot)
        for p in range(2):
            column = jnp.transpose(jnp.broadcast_to(corr_ref[p : p + 1, :], (rows, rows)))
            column = jnp.concatenate([column] * (pair_ref.shape[1] // rows), 1)
            pair = pair_ref[...]
            norm[p] = 1.0 / (root * jnp.sqrt(1.0 + column * column + pair * pair))

    def pick():
        get_first().wait()
        for q in range(2):
            span = part_of(q)
            for j in range(16):
                spot = ids[j] - r * rows
                here = jnp.logical_and(spot >= 0, spot < rows)
                row = first[pl.ds(jnp.clip(spot, 0, rows - 1), 1), span]
                mine[j, :, span] = jnp.where(here, row, jnp.zeros_like(row))

    pltpu.make_async_copy(blocks.at[0], blocks.at[0], load_s.at[0]).wait()
    pl.semaphore_wait(barrier, len(peers))

    for step in OPENING:
        if isinstance(step, int):
            turn(step)
        elif step == ():
            pick()
        elif step == (0,):
            prepare()
        else:
            p_stage(*step)

    def index_of(p, d, e):
        return 2 * (((w + e) % 2) * 4 + (z + d) % 4) + p

    def build(slot, t, js):
        span = chunk_of(t)
        for n, j in enumerate(js):
            up, down = halves(first[:, span] * pivots[j, :, span])
            scaled[slot, n * rows : (n + 1) * rows, :size] = up
            scaled[slot, n * rows : (n + 1) * rows, size:] = down

    def product(slot, t, count):
        left = scaled[slot, : count * rows]
        up, down = high[t], low[t]
        left = jnp.concatenate([left, left[:, :size]], 1)
        right = jnp.concatenate([up, up, down], 1)
        return lax.dot_general(left, right, NT, preferred_element_type=F32)

    def main(t, carry):
        turn(2 * t + AHEAD)
        turn(2 * t + AHEAD + 1)

        for when, stage in ((1, 5), (2, 6)):

            @pl.when(t == when)
            def _():
                p_stage(1, stage)

        for n in range(16):
            a, b, k = n // 4, (n // 2) % 2, n % 2
            for m in range(2):
                up, down = halves(blocks[2 * t + m, k, a, b])
                high[t, n * 16 : (n + 1) * 16, m * small : (m + 1) * small] = up
                low[t, n * 16 : (n + 1) * 16, m * small : (m + 1) * small] = down
        for g, group in enumerate(EARLY):
            build(g, t, [index_of(p, d, e) for p, d in group for e in range(2)])
            result = product(g, t, 2 * len(group))
            for m, (p, d) in enumerate(group):
                for e in range(2):
                    lo = (2 * m + e) * rows
                    tot[p, d, e] += result[lo : lo + rows]

        return carry

    lax.fori_loop(0, CHUNKS, main, 0)

    half = rows // 2

    def r_copy(p, n, src, dst, peer, lane=0):
        return pltpu.make_async_remote_copy(
            src_ref=src,
            dst_ref=dst,
            send_sem=r_send.at[p, lane],
            recv_sem=r_recv.at[p, n],
            device_id=peer,
            device_id_type=MESH,
        )

    def f_copies():
        return [r_copy(0, n, tot.at[0, d, 1], side.at[d], to_w) for n, d in enumerate((2, 3, 1, 0))] + [
            r_copy(0, 4, tot.at[0, 2, 0, pl.ds(0, half)], hop1.at[0, 0, 0], z_up, 1),
            r_copy(0, 5, tot.at[0, 2, 0, pl.ds(half, half)], hop1.at[0, 1, 0], z_down, 1),
            r_copy(0, 6, tot.at[0, 1, 0], hop2.at[0, 0, 0], z_up, 1),
            r_copy(0, 7, tot.at[0, 3, 0], hop2.at[0, 1, 0], z_down, 1),
        ]

    def r_copies():
        return (
            r_copy(1, 0, tot.at[1, 2, :, pl.ds(0, half)], hop1.at[1, 0], z_up),
            r_copy(1, 1, tot.at[1, 2, :, pl.ds(half, half)], hop1.at[1, 1], z_down),
            r_copy(1, 2, tot.at[1, 1, 1], hop2.at[1, 0, 1], z_up),
            r_copy(1, 3, tot.at[1, 3, 1], hop2.at[1, 1, 1], z_down),
            r_copy(1, 4, tot.at[1, 1, 0], hop2.at[1, 0, 0], z_up),
            r_copy(1, 5, tot.at[1, 3, 0], hop2.at[1, 1, 0], z_down),
            r_copy(1, 6, part, far_side, to_w, 1),
        )

    def fold_out():
        for copy in f_copies()[:4]:
            copy.start()

    def fold_in(n):
        d = (2, 3, 1, 0)[n]
        copies = f_copies()
        copies[n].wait_recv()
        tot[0, d, 0] += side[d]
        if n == 0:
            copies[4].start()
            copies[5].start()
        if n in (1, 2):
            way = 2 - n
            copies[4 + way].wait_recv()
            tot[0, d, 0, way * half : (way + 1) * half] += hop1[0, way, 0]
            copies[6 + way].start()

    def far_out():
        copies = r_copies()
        copies[0].start()
        copies[1].start()

    def near_out(way):
        copies = r_copies()
        copies[way].wait_recv()
        d = (1, 3)[way]
        tot[1, d, :, way * half : (way + 1) * half] += hop1[1, way]
        copies[2 + way].start()
        copies[4 + way].start()

    def pair_out():
        copies = r_copies()
        copies[2].wait_recv()
        copies[3].wait_recv()
        part[...] = tot[1, 0, 1] + hop2[1, 0, 1] + hop2[1, 1, 1]
        copies[6].start()

    def put_out(p):
        return pltpu.make_async_copy(norm.at[p], out_hbm.at[p], load_f.at[p])

    def finish(p):
        copies = (f_copies(), r_copies())[p]
        for n in ((6, 7), (4, 5))[p]:
            copies[n].wait_recv()
        total = tot[p, 0, 0] + hop2[p, 0, 0] + hop2[p, 1, 0]
        if p == 1:
            copies[6].wait_recv()
            total = total + far_side[...]
        norm[p] = total * norm[p]
        put_out(p).start()

    def second_pass(d):
        js = [index_of(1, d, e) for e in range(2)]

        def body(u, carry):
            for g in range(2):
                t = 2 * u + g
                build(g, t, js)
                result = product(g, t, 2)
                for e in range(2):
                    tot[1, d, e] += result[e * rows : (e + 1) * rows]
            return carry

        lax.fori_loop(0, CHUNKS // 2, body, 0)

    fold_out()
    far_out()
    second_pass(1)
    fold_in(0)
    near_out(0)
    near_out(1)
    second_pass(0)
    fold_in(1)
    fold_in(2)
    for t in (0, 8):
        all_sent = blocks.at[pl.ds(0, 15), 0]
        s_copy(t, 0, all_sent, to_core).wait_send()
    rows_sent = blocks.at[pl.ds(0, 15), 0, 0]
    p_copy(0, 0, rows_sent, rows_sent, to_core).wait_send()
    fold_in(3)
    pair_out()
    finish(0)
    finish(1)
    for p, lane, sent in (
        (0, 0, side),
        (0, 1, side.at[pl.ds(0, 3)]),
        (1, 0, tot.at[0, pl.ds(0, 3)]),
        (1, 1, part),
    ):
        r_copy(p, 0, sent, sent, to_core, lane).wait_send()
    for p in range(2):
        put_out(p).wait()


def shards(first_profiles, second_profiles, pivot_ids, pivot_corr, pair_corr):
    n_cols = lax.axis_size("cols")
    rows, samples = first_profiles.shape
    second_rows = second_profiles.shape[0]
    width = pair_corr.shape[1]
    size = samples // CHUNKS
    small = samples // SMALL
    root = math.sqrt(float(samples * n_cols))
    vmem = pl.BlockSpec(memory_space=pltpu.VMEM)
    hbm = pl.BlockSpec(memory_space=pl.ANY)
    dma = pltpu.SemaphoreType.DMA
    return pl.pallas_call(
        functools.partial(kernel, root),
        out_shape=jax.ShapeDtypeStruct((2, rows, width), F32),
        in_specs=[pl.BlockSpec(memory_space=pltpu.SMEM), hbm, hbm, vmem, vmem],
        out_specs=hbm,
        scratch_shapes=[
            pltpu.VMEM((rows, samples), F32),
            pltpu.VMEM((SMALL, 2, 4, 2, second_rows, small), F32),
            pltpu.VMEM((CHUNKS, width, size), BF16),
            pltpu.VMEM((CHUNKS, width, size), BF16),
            pltpu.VMEM((3, 4 * rows, 2 * size), BF16),
            pltpu.VMEM((2, 4, 2, rows, width), F32),
            pltpu.VMEM((2, 2, 2, rows // 2, width), F32),
            pltpu.VMEM((2, 2, 2, rows, width), F32),
            pltpu.VMEM((4, rows, width), F32),
            pltpu.VMEM((rows, width), F32),
            pltpu.VMEM((rows, width), F32),
            pltpu.VMEM((2, rows, width), F32),
            pltpu.VMEM((16, 1, samples), F32),
            pltpu.VMEM((8, 1, samples), F32),
            pltpu.VMEM((8, 1, samples), F32),
            pltpu.VMEM((4, 1, samples), F32),
            pltpu.VMEM((4, 1, samples), F32),
            pltpu.VMEM((4, 1, samples), F32),
            pltpu.VMEM((16, 1, samples), F32),
            dma((2,)),
            dma((1,)),
            dma((2,)),
            dma((SMALL, 6)),
            dma((1,)),
            dma((2, 6)),
            dma((2, 2)),
            dma((2, 8)),
        ],
        compiler_params=pltpu.CompilerParams(
            collective_id=0, has_side_effects=True, vmem_limit_bytes=56 * 2**20
        ),
        name="comoments",
    )(pivot_ids, first_profiles, second_profiles, pivot_corr, pair_corr)


def solution(mesh):
    in_specs = (P("rows", "cols"), P("rows", "cols"), P(), P("cols", "rows"), P("rows", None))
    out_specs = P("cols", "rows", None)
    return jax.shard_map(shards, mesh=mesh, in_specs=in_specs, out_specs=out_specs, check_vma=False)
```

```python
import functools
import math

import jax
import jax.numpy as jnp
from jax import lax
from jax.experimental import pallas as pl
from jax.experimental.pallas import tpu as pltpu
from jax.sharding import PartitionSpec as P

MESH = pl.DeviceIdType.MESH
F32 = jnp.float32
BF16 = jnp.bfloat16
NT = (((1,), (1,)), ((), ()))
CHUNKS = 8
SMALL = 16
LAGS = ((3, 2), (5, 3), (0, 0), (3, 1), (8, 4), (10, 5))
AHEAD = 10
OPENING = (
    *(0, 1, 2, (), (0, 0), (1, 0), (0, 1), (1, 1), (0,), 3),
    *((0, 2), 4, 5, (0, 3), (1, 2), 6, 7, (0, 4), (1, 3)),
    *(8, (0, 5), 9, (1, 4), (0, 6)),
)
GROUP = (0, 1, 1, 2, 2, 3, 3, 4, 5)
PARTS = ((0, 2), (2, 6))
EARLY = (((0, 2), (0, 1)), ((0, 3), (0, 0)), ((1, 2), (1, 3)))


def halves(x):
    high = x.astype(BF16)
    return high, (x - high.astype(F32)).astype(BF16)


def kernel(
    root,
    ids,
    first_hbm,
    second_hbm,
    corr_ref,
    pair_ref,
    out_hbm,
    first,
    blocks,
    high,
    low,
    scaled,
    tot,
    hop1,
    hop2,
    side,
    far_side,
    part,
    norm,
    mine,
    other,
    merged,
    second,
    near,
    gathered,
    pivots,
    load_f,
    load_s,
    s_send,
    s_recv,
    p_send,
    p_recv,
    r_send,
    r_recv,
):
    r, c = lax.axis_index("rows"), lax.axis_index("cols")
    core, chip = r % 2, r // 2
    x, y = chip // 2, chip % 2
    z, w = c % 4, c // 4
    rows, samples = first_hbm.shape
    size = samples // CHUNKS
    small = samples // SMALL

    def at_chip(other_chip, other_core=None):
        return (other_chip * 2 + (core if other_core is None else other_core), c)

    x_up, x_down, x_far = (x + 1) % 4, (x + 3) % 4, (x + 2) % 4
    to_y = at_chip(x * 2 + 1 - y)
    to_up = at_chip(x_up * 2 + y)
    to_down = at_chip(x_down * 2 + y)
    to_core = at_chip(chip, 1 - core)
    z_up = (r, w * 4 + (z + 1) % 4)
    z_down = (r, w * 4 + (z + 3) % 4)
    to_w = (r, (1 - w) * 4 + z)

    def part_of(q):
        return pl.ds(PARTS[q][0] * size, PARTS[q][1] * size)

    def chunk_of(t):
        return pl.ds(pl.multiple_of(t * size, 128), size)

    def get_first():
        return pltpu.make_async_copy(first_hbm, first, load_f.at[0])

    def get_second(t):
        return pltpu.make_async_copy(
            second_hbm.at[:, pl.ds(pl.multiple_of(t * small, 128), small)], blocks.at[t, core, x, y], load_s.at[0]
        )

    for t in range(SMALL):
        get_second(t).start()
    get_first().start()

    barrier = pltpu.get_barrier_semaphore()
    to_far = at_chip(x_far * 2 + y)
    peers = [to_core, to_y, to_up, to_down, to_far, z_up, z_down, to_w]
    for peer in peers:
        pl.semaphore_signal(barrier, inc=1, device_id=peer, device_id_type=MESH)

    def s_copy(t, n, ref, peer):
        return pltpu.make_async_remote_copy(
            src_ref=ref,
            dst_ref=ref,
            send_sem=s_send.at[t // 8],
            recv_sem=s_recv.at[t, GROUP[n]],
            device_id=peer,
            device_id_type=MESH,
        )

    def s_copies(t):
        own = blocks.at[t, core, x, y]
        pair = blocks.at[t, core, x, 1 - y]
        far = blocks.at[t, core, x_far, y]
        half = own.shape[0] // 2
        return (
            s_copy(t, 0, own, to_y),
            s_copy(t, 1, own, to_up),
            s_copy(t, 2, own, to_down),
            s_copy(t, 3, pair, to_up),
            s_copy(t, 4, pair, to_down),
            s_copy(t, 5, blocks.at[t, core, x_down, y, pl.ds(0, half)], to_up),
            s_copy(t, 6, blocks.at[t, core, x_up, y, pl.ds(half, half)], to_down),
            s_copy(t, 7, far, to_y),
            s_copy(t, 8, blocks.at[t, core], to_core),
        )

    def s_stage(t, stage):
        copies = s_copies(t)
        starts = ((0, 1, 2), (3, 4), (5, 6), (7,), (8,), ())[stage]
        landed = (
            (),
            ((0, blocks.at[t, core, x, 1 - y]),),
            ((1, blocks.at[t, core, x]),),
            ((5, blocks.at[t, core, x_far, y]),),
            ((3, blocks.at[t, core, x]), (7, blocks.at[t, core, x_far, 1 - y])),
            ((8, blocks.at[t, 1 - core]),),
        )[stage]
        for arrival in landed:
            s_copy(t, *arrival, to_core).wait_recv()
        for n in starts:
            copies[n].start()

    def turn(n):
        for lag, stage in LAGS:
            t = n - lag
            if isinstance(t, int):
                if 0 <= t < SMALL:
                    s_stage(t, stage)
            else:

                @pl.when(jnp.logical_and(t >= 0, t < SMALL))
                def _():
                    s_stage(t, stage)

    def p_copy(q, n, src, dst, peer):
        return pltpu.make_async_remote_copy(
            src_ref=src,
            dst_ref=dst,
            send_sem=p_send.at[0],
            recv_sem=p_recv.at[q, n],
            device_id=peer,
            device_id_type=MESH,
        )

    def p_copies(q):
        span = part_of(q)
        spread, gather = [], []
        row = pivots.at[8 * core + 4 * y + x, :, span]
        for i in range(1, 4):
            there = (x + i) % 4
            peer = at_chip(there * 2 + y)
            spread.append(p_copy(q, 2, near.at[there, :, span], gathered.at[i, :, span], peer))
            gather.append(p_copy(q, 3, row, row, peer))
        pair_rows = pivots.at[pl.ds(8 * core + 4 * y, 4), :, span]
        core_rows = pivots.at[pl.ds(8 * core, 8), :, span]
        return (
            [p_copy(q, 0, mine.at[pl.ds(8 * (1 - core), 8), :, span], other.at[:, :, span], to_core)],
            [p_copy(q, 1, merged.at[pl.ds(4 * (1 - y), 4), :, span], second.at[:, :, span], to_y)],
            spread,
            gather,
            [p_copy(q, 4, pair_rows, pair_rows, to_y)],
            [p_copy(q, 5, core_rows, core_rows, to_core)],
        )

    def p_stage(q, stage):
        copies = p_copies(q)
        span = part_of(q)
        if stage > 0:
            if stage in (3, 4):
                three = gathered.at[pl.ds(1, 3), :, span]
                p_copy(q, stage - 1, three, three, to_core).wait_recv()
            else:
                copies[stage - 1][0].wait_recv()
        if stage == 1:
            merged[:, :, span] = mine[pl.ds(8 * core, 8), :, span] + other[:, :, span]
        elif stage == 2:
            near[:, :, span] = merged[pl.ds(4 * y, 4), :, span] + second[:, :, span]
        elif stage == 3:
            total = near[x, :, span]
            for i in range(1, 4):
                total = total + gathered[i, :, span]
            pivots[8 * core + 4 * y + x, :, span] = total
        if stage < 6:
            for copy in copies[stage]:
                copy.start()

    def prepare():
        tot[...] = jnp.zeros_like(tot)
        for p in range(2):
            column = jnp.transpose(jnp.broadcast_to(corr_ref[p : p + 1, :], (rows, rows)))
            column = jnp.concatenate([column] * (pair_ref.shape[1] // rows), 1)
            pair = pair_ref[...]
            norm[p] = 1.0 / (root * jnp.sqrt(1.0 + column * column + pair * pair))

    def pick():
        get_first().wait()
        for q in range(2):
            span = part_of(q)
            for j in range(16):
                spot = ids[j] - r * rows
                here = jnp.logical_and(spot >= 0, spot < rows)
                row = first[pl.ds(jnp.clip(spot, 0, rows - 1), 1), span]
                mine[j, :, span] = jnp.where(here, row, jnp.zeros_like(row))

    pltpu.make_async_copy(blocks.at[0], blocks.at[0], load_s.at[0]).wait()
    pl.semaphore_wait(barrier, len(peers))

    for step in OPENING:
        if isinstance(step, int):
            turn(step)
        elif step == ():
            pick()
        elif step == (0,):
            prepare()
        else:
            p_stage(*step)

    def index_of(p, d, e):
        return 2 * (((w + e) % 2) * 4 + (z + d) % 4) + p

    def build(slot, t, js):
        span = chunk_of(t)
        for n, j in enumerate(js):
            up, down = halves(first[:, span] * pivots[j, :, span])
            scaled[slot, n * rows : (n + 1) * rows, :size] = up
            scaled[slot, n * rows : (n + 1) * rows, size:] = down

    def product(slot, t, count):
        left = scaled[slot, : count * rows]
        up, down = high[t], low[t]
        left = jnp.concatenate([left, left[:, :size]], 1)
        right = jnp.concatenate([up, up, down], 1)
        return lax.dot_general(left, right, NT, preferred_element_type=F32)

    def main(t, carry):
        turn(2 * t + AHEAD)
        turn(2 * t + AHEAD + 1)

        for when, stage in ((1, 5), (2, 6)):

            @pl.when(t == when)
            def _():
                p_stage(1, stage)

        for n in range(16):
            a, b, k = n // 4, (n // 2) % 2, n % 2
            for m in range(2):
                up, down = halves(blocks[2 * t + m, k, a, b])
                high[t, n * 16 : (n + 1) * 16, m * small : (m + 1) * small] = up
                low[t, n * 16 : (n + 1) * 16, m * small : (m + 1) * small] = down
        for g, group in enumerate(EARLY):
            build(g, t, [index_of(p, d, e) for p, d in group for e in range(2)])
            result = product(g, t, 2 * len(group))
            for m, (p, d) in enumerate(group):
                for e in range(2):
                    lo = (2 * m + e) * rows
                    tot[p, d, e] += result[lo : lo + rows]

        return carry

    lax.fori_loop(0, CHUNKS, main, 0)

    half = rows // 2

    def r_copy(p, n, src, dst, peer, lane=0):
        return pltpu.make_async_remote_copy(
            src_ref=src,
            dst_ref=dst,
            send_sem=r_send.at[p, lane],
            recv_sem=r_recv.at[p, n],
            device_id=peer,
            device_id_type=MESH,
        )

    def f_copies():
        return [r_copy(0, n, tot.at[0, d, 1], side.at[d], to_w) for n, d in enumerate((2, 3, 1, 0))] + [
            r_copy(0, 4, tot.at[0, 2, 0, pl.ds(0, half)], hop1.at[0, 0, 0], z_up, 1),
            r_copy(0, 5, tot.at[0, 2, 0, pl.ds(half, half)], hop1.at[0, 1, 0], z_down, 1),
            r_copy(0, 6, tot.at[0, 1, 0], hop2.at[0, 0, 0], z_up, 1),
            r_copy(0, 7, tot.at[0, 3, 0], hop2.at[0, 1, 0], z_down, 1),
        ]

    def r_copies():
        return (
            r_copy(1, 0, tot.at[1, 2, :, pl.ds(0, half)], hop1.at[1, 0], z_up),
            r_copy(1, 1, tot.at[1, 2, :, pl.ds(half, half)], hop1.at[1, 1], z_down),
            r_copy(1, 2, tot.at[1, 1, 1], hop2.at[1, 0, 1], z_up),
            r_copy(1, 3, tot.at[1, 3, 1], hop2.at[1, 1, 1], z_down),
            r_copy(1, 4, tot.at[1, 1, 0], hop2.at[1, 0, 0], z_up),
            r_copy(1, 5, tot.at[1, 3, 0], hop2.at[1, 1, 0], z_down),
            r_copy(1, 6, part, far_side, to_w, 1),
        )

    def fold_out():
        for copy in f_copies()[:4]:
            copy.start()

    def fold_in(n):
        d = (2, 3, 1, 0)[n]
        copies = f_copies()
        copies[n].wait_recv()
        tot[0, d, 0] += side[d]
        if n == 0:
            copies[4].start()
            copies[5].start()
        if n in (1, 2):
            way = 2 - n
            copies[4 + way].wait_recv()
            tot[0, d, 0, way * half : (way + 1) * half] += hop1[0, way, 0]
            copies[6 + way].start()

    def far_out():
        copies = r_copies()
        copies[0].start()
        copies[1].start()

    def near_out(way):
        copies = r_copies()
        copies[way].wait_recv()
        d = (1, 3)[way]
        tot[1, d, :, way * half : (way + 1) * half] += hop1[1, way]
        copies[2 + way].start()
        copies[4 + way].start()

    def pair_out():
        copies = r_copies()
        copies[2].wait_recv()
        copies[3].wait_recv()
        part[...] = tot[1, 0, 1] + hop2[1, 0, 1] + hop2[1, 1, 1]
        copies[6].start()

    def put_out(p):
        return pltpu.make_async_copy(norm.at[p], out_hbm.at[p], load_f.at[p])

    def finish(p):
        copies = (f_copies(), r_copies())[p]
        for n in ((6, 7), (4, 5))[p]:
            copies[n].wait_recv()
        total = tot[p, 0, 0] + hop2[p, 0, 0] + hop2[p, 1, 0]
        if p == 1:
            copies[6].wait_recv()
            total = total + far_side[...]
        norm[p] = total * norm[p]
        put_out(p).start()

    def second_pass(d):
        js = [index_of(1, d, e) for e in range(2)]

        def body(u, carry):
            for g in range(4):
                t = 4 * u + g
                build(g % 3, t, js)
                result = product(g % 3, t, 2)
                for e in range(2):
                    tot[1, d, e] += result[e * rows : (e + 1) * rows]
            return carry

        lax.fori_loop(0, CHUNKS // 4, body, 0)

    fold_out()
    far_out()
    second_pass(1)
    fold_in(0)
    near_out(0)
    near_out(1)
    second_pass(0)
    fold_in(1)
    fold_in(2)
    for t in (0, 8):
        all_sent = blocks.at[pl.ds(0, 15), 0]
        s_copy(t, 0, all_sent, to_core).wait_send()
    rows_sent = blocks.at[pl.ds(0, 15), 0, 0]
    p_copy(0, 0, rows_sent, rows_sent, to_core).wait_send()
    fold_in(3)
    pair_out()
    finish(0)
    finish(1)
    for p, lane, sent in (
        (0, 0, side),
        (0, 1, side.at[pl.ds(0, 3)]),
        (1, 0, tot.at[0, pl.ds(0, 3)]),
        (1, 1, part),
    ):
        r_copy(p, 0, sent, sent, to_core, lane).wait_send()
    for p in range(2):
        put_out(p).wait()


def shards(first_profiles, second_profiles, pivot_ids, pivot_corr, pair_corr):
    n_cols = lax.axis_size("cols")
    rows, samples = first_profiles.shape
    second_rows = second_profiles.shape[0]
    width = pair_corr.shape[1]
    size = samples // CHUNKS
    small = samples // SMALL
    root = math.sqrt(float(samples * n_cols))
    vmem = pl.BlockSpec(memory_space=pltpu.VMEM)
    hbm = pl.BlockSpec(memory_space=pl.ANY)
    dma = pltpu.SemaphoreType.DMA
    return pl.pallas_call(
        functools.partial(kernel, root),
        out_shape=jax.ShapeDtypeStruct((2, rows, width), F32),
        in_specs=[pl.BlockSpec(memory_space=pltpu.SMEM), hbm, hbm, vmem, vmem],
        out_specs=hbm,
        scratch_shapes=[
            pltpu.VMEM((rows, samples), F32),
            pltpu.VMEM((SMALL, 2, 4, 2, second_rows, small), F32),
            pltpu.VMEM((CHUNKS, width, size), BF16),
            pltpu.VMEM((CHUNKS, width, size), BF16),
            pltpu.VMEM((3, 4 * rows, 2 * size), BF16),
            pltpu.VMEM((2, 4, 2, rows, width), F32),
            pltpu.VMEM((2, 2, 2, rows // 2, width), F32),
            pltpu.VMEM((2, 2, 2, rows, width), F32),
            pltpu.VMEM((4, rows, width), F32),
            pltpu.VMEM((rows, width), F32),
            pltpu.VMEM((rows, width), F32),
            pltpu.VMEM((2, rows, width), F32),
            pltpu.VMEM((16, 1, samples), F32),
            pltpu.VMEM((8, 1, samples), F32),
            pltpu.VMEM((8, 1, samples), F32),
            pltpu.VMEM((4, 1, samples), F32),
            pltpu.VMEM((4, 1, samples), F32),
            pltpu.VMEM((4, 1, samples), F32),
            pltpu.VMEM((16, 1, samples), F32),
            dma((2,)),
            dma((1,)),
            dma((2,)),
            dma((SMALL, 6)),
            dma((1,)),
            dma((2, 6)),
            dma((2, 2)),
            dma((2, 8)),
        ],
        compiler_params=pltpu.CompilerParams(
            collective_id=0, has_side_effects=True, vmem_limit_bytes=56 * 2**20
        ),
        name="comoments",
    )(pivot_ids, first_profiles, second_profiles, pivot_corr, pair_corr)


def solution(mesh):
    in_specs = (P("rows", "cols"), P("rows", "cols"), P(), P("cols", "rows"), P("rows", None))
    out_specs = P("cols", "rows", None)
    return jax.shard_map(shards, mesh=mesh, in_specs=in_specs, out_specs=out_specs, check_vma=False)
```
